32 devices in a mesh: mesh: 16 (over z, y, core), band: 2 (over x).
Axes of the slice: x: 2, y: 2, z: 4, core: 2. Of those that a mesh axis runs over, the one named last changes fastest.
Arguments:
- psi: bfloat16 [16, 286720], P('band', 'mesh'), may hold values from -9 to 9
- cell_nodes: int32 [216, 128], replicated, may hold values from 0 to 19711, as said below
- cell_scale: float32 [2048], P('mesh'), may hold values from 0.5 to 2
- cell_matrix: bfloat16 [216, 216], replicated, may hold values from -1 to 2
- node_potential: bfloat16 [286720], P('mesh'), may hold values from -1.5 to 0.5
- proj_values: bfloat16 [216, 8, 2048], P(None, None, 'mesh'), may hold values from -1 to 1
- entry_cell: int32 [2048], P('mesh'), may hold values from 0 to 127
- entry_atom: int32 [2048], P('mesh'), may hold values from -1 to 191, as said below
- coupling: float32 [1024, 8, 8], P('mesh'), may hold values from -3 to 3
Outputs:
- filtered: bfloat16 [16, 286720], P('band', 'mesh')
- correlation: float32 [16, 16], replicated
The draws below stay inside these ranges and needn't reach their ends.
Inputs may be any that keep to these rules, and one draw needn't show every extreme that they name: `cell_nodes`: node j = 36 a + 6 b + c of a cell is its local node (a, b, c) in the order the cell_matrix uses; cells that share a node give it the same number; values 17920 + i name node i of the next partition, and only nodes below 1792 of a partition are named so by the previous one. `entry_atom`: live entries of a partition come first, then -1 padding; the number of live entries differs between partitions.
All inputs are finite; a program needn't handle non-finite values.
Results may differ from the reference program's by a relative error of at most 0.0022.
Values may be sent and summed in bfloat16 or wider, within the bound.
A program may use at most 128 MiB of HBM per device.

```python
import math
import jax
import jax.numpy as jnp
from jax import lax

STATES = 16
NPROJ = 8
CROSS = 8
ATOMS = 64
ENTRIES = 128
FACEP = 1792
NODES = 17920
CELLS = 128
NODES_ALL = 286720
CELLS_ALL = 2048
ENTRIES_ALL = 2048
ATOMS_ALL = 1024
N_MESH = 16


def draw_psi(key, part):
    ramp = 0.5 * (1.0 + 2.0 * jnp.arange(NODES_ALL, dtype=jnp.float32) / NODES_ALL)
    values = jnp.clip(jax.random.normal(jax.random.fold_in(key, 13), (STATES, NODES_ALL), jnp.float32), -6.0, 6.0)
    return (values * ramp[None, :]).astype(jnp.bfloat16)


def draw_cell_matrix(key, part):
    noise_vals = jnp.clip(jax.random.normal(jax.random.fold_in(key, 22), (216, 216), jnp.float32) * 0.048, -0.2, 0.2)
    matrix = jnp.eye(216, dtype=jnp.float32) + noise_vals + noise_vals.T
    return matrix.astype(jnp.bfloat16)


def draw_cell_nodes(key, part):
    side = 5 * CROSS + 1
    cell_ids = jnp.arange(CELLS, dtype=jnp.int32)
    cell_x = cell_ids // (CROSS * CROSS)
    cell_y = cell_ids // CROSS % CROSS
    cell_z = cell_ids % CROSS
    local_ids = jnp.arange(216, dtype=jnp.int32)
    local_a = local_ids // 36
    local_b = local_ids // 6 % 6
    local_c = local_ids % 6
    layer = 5 * cell_x[None, :] + local_a[:, None]
    across = (5 * cell_y[None, :] + local_b[:, None]) * side + 5 * cell_z[None, :] + local_c[:, None]
    shuffled = 1 + jax.random.permutation(jax.random.fold_in(key, 31), FACEP - 2).astype(jnp.int32)
    position = jnp.concatenate([jnp.array([FACEP - 1, 0], jnp.int32), shuffled])
    base_table = layer * FACEP + position[across]
    order = jax.random.permutation(jax.random.fold_in(key, 32), CELLS).astype(jnp.int32)
    table = base_table[:, order]
    return table.astype(jnp.int32)


def draw_entry_atom(key, part):
    partitions = ENTRIES_ALL // ENTRIES
    live_count = jax.random.randint(jax.random.fold_in(key, 41), (partitions,), ENTRIES // 4, ENTRIES + 1)
    live_count = live_count.at[0].set(ENTRIES).at[partitions - 1].set(ENTRIES // 2)
    slot_vals = jax.random.randint(jax.random.fold_in(key, 42), (partitions, ENTRIES), 0, 3 * ATOMS)
    slot_vals = slot_vals.at[0, 0].set(3 * ATOMS - 1)
    places = jnp.arange(ENTRIES, dtype=jnp.int32)
    result = jnp.where(places[None, :] < live_count[:, None], slot_vals, -1)
    return result.reshape(ENTRIES_ALL).astype(jnp.int32)


def with_ends(entries, stream_key, low, top_value):
    spot = [jax.random.randint(jax.random.fold_in(stream_key, axis), (), 0, length) for axis, length in enumerate(entries.shape)]
    main_axis = entries.shape.index(max(entries.shape))
    beside = spot[:main_axis] + [(spot[main_axis] + 1) % entries.shape[main_axis]] + spot[main_axis + 1:]
    return entries.at[tuple(spot)].set(low).at[tuple(beside)].set(top_value)


def steps_of(stream_key, shape, pieces, least, largest):
    level = 1.0
    for axis_at, shards_of in pieces:
        draws = jax.random.uniform(jax.random.fold_in(jax.random.fold_in(stream_key, 6), axis_at), (shards_of,), jnp.float32, least / len(pieces), largest / len(pieces))
        level = level * jnp.repeat(jnp.exp(draws), shape[axis_at] // shards_of).reshape((-1,) + (1,) * (len(shape) - 1 - axis_at))
    return level


def bell_draw(key, dims, deviation, bound, split=(), held_as=jnp.bfloat16):
    entries = deviation * jax.random.normal(key, dims, jnp.float32)
    if split:
        entries = entries * steps_of(key, dims, split, -0.22, 0.18)
    return jnp.clip(entries, -bound, bound).astype(held_as)


def setup_inputs(seed: int = 0) -> dict:
    streams_of = jax.random.split(jax.random.key(seed), 10)
    return {
        "psi": draw_psi(jax.random.fold_in(streams_of[9], 71), 0),
        "cell_nodes": draw_cell_nodes(jax.random.fold_in(streams_of[9], 71), 0),
        "cell_scale": jnp.clip(jnp.exp(math.log(2.0) - 1.3862944 * jax.random.uniform(streams_of[2], (CELLS_ALL,), jnp.float32) ** steps_of(streams_of[2], (CELLS_ALL,), ((0, 16),), -0.2, 0.2)), 0.5, 2.0),
        "cell_matrix": draw_cell_matrix(jax.random.fold_in(streams_of[9], 71), 0),
        "node_potential": jnp.clip(-1.5 + 2.0 * jax.random.uniform(streams_of[4], (NODES_ALL,), jnp.float32) ** steps_of(streams_of[4], (NODES_ALL,), ((0, 16),), -0.2, 0.2), -1.5, 0.5).astype(jnp.bfloat16),
        "proj_values": bell_draw(streams_of[5], (216, NPROJ, ENTRIES_ALL), 0.15, 1.0, ((2, 16),)),
        "entry_cell": with_ends(jax.random.randint(streams_of[6], (ENTRIES_ALL,), 0, CELLS), jax.random.fold_in(streams_of[6], 1), 0, CELLS - 1).astype(jnp.int32),
        "entry_atom": draw_entry_atom(jax.random.fold_in(streams_of[9], 71), 0),
        "coupling": bell_draw(streams_of[8], (ATOMS_ALL, NPROJ, NPROJ), 0.5, 3.0, ((0, 16),), jnp.float32),
    }


CENTER = 0.5
HALFWIDTH = 2.5
HIGH = lax.Precision.HIGHEST


def one_hot(entry_slots):
    slot_ids = jnp.arange(3 * ATOMS, dtype=jnp.int32)
    return (entry_slots[:, None] == slot_ids[None, :]).astype(jnp.float32)


def finish(summed, field, potential, base_field, second):
    scaled = (summed + (potential.astype(jnp.float32) - CENTER) * field.astype(jnp.float32)) / HALFWIDTH
    if second:
        return (2.0 * scaled - base_field.astype(jnp.float32)).astype(jnp.bfloat16)
    return scaled.astype(jnp.bfloat16)


def reference(psi, cell_nodes, cell_scale, cell_matrix, node_potential, proj_values, entry_cell, entry_atom, coupling):
    partitions = N_MESH
    states = psi.shape[0]
    local_width = cell_nodes.shape[0]
    fields = psi.reshape(states, partitions, NODES).transpose(1, 0, 2)
    cell_list = cell_nodes
    scale_rows = cell_scale.reshape(partitions, CELLS)
    potentials = node_potential.reshape(partitions, NODES)
    projectors = proj_values.reshape(local_width, NPROJ, partitions, ENTRIES).transpose(2, 0, 1, 3)
    entry_cells = entry_cell.reshape(partitions, ENTRIES)
    entry_slots = entry_atom.reshape(partitions, ENTRIES)
    couplings = coupling.reshape(partitions, ATOMS, NPROJ, NPROJ)
    kernel = cell_matrix.astype(jnp.float32)

    def partial_terms(items):
        field, ghost, project, ecells, eslots = items
        extended = jnp.concatenate([field, ghost], axis=1)
        values = extended[:, cell_list[:, ecells]].astype(jnp.float32)
        partial_sum = jnp.einsum("jke,sje->esk", project.astype(jnp.float32), values, precision=HIGH)
        partial_sum = partial_sum.reshape(ENTRIES, states * NPROJ)
        grouped = jnp.dot(one_hot(eslots).T, partial_sum, precision=HIGH)
        return grouped.reshape(3, ATOMS, states * NPROJ)

    def make_assemble(second):
        def assemble(items):
            field, ghost, scales, project, ecells, eslots, beside_all, potential, base_field = items
            extended = jnp.concatenate([field, ghost], axis=1)
            cell_vals = extended[:, cell_list].astype(jnp.float32)
            cell_terms = jnp.einsum("ij,sjc->sic", kernel, cell_vals, precision=HIGH) * scales
            entry_terms = jnp.dot(one_hot(eslots), beside_all, precision=HIGH).reshape(ENTRIES, states, NPROJ)
            node_terms = jnp.einsum("jke,esk->sje", project.astype(jnp.float32), entry_terms, precision=HIGH)
            summed = jnp.zeros((states, NODES + FACEP), jnp.float32)
            summed = summed.at[:, cell_list].add(cell_terms)
            summed = summed.at[:, cell_list[:, ecells]].add(node_terms)
            tail = finish(summed[:, FACEP:NODES], field[:, FACEP:], potential[None, FACEP:], base_field[:, FACEP:], second)
            return tail, summed[:, :FACEP], summed[:, NODES:]
        return assemble

    def apply_filter(field_all, base_all, second):
        ghosts = jnp.roll(field_all[:, :, :FACEP], -1, axis=0)
        grouped = lax.map(partial_terms, (field_all, ghosts, projectors, entry_cells, entry_slots))
        coefficient = grouped[:, 1] + jnp.roll(grouped[:, 2], 1, axis=0) + jnp.roll(grouped[:, 0], -1, axis=0)
        coefficient = coefficient.reshape(partitions, ATOMS, states, NPROJ)
        atom_vals = jnp.einsum("pakl,pasl->pask", couplings, coefficient, precision=HIGH)
        atom_vals = atom_vals.reshape(partitions, ATOMS, states * NPROJ)
        beside_all = jnp.concatenate([jnp.roll(atom_vals, 1, axis=0), atom_vals, jnp.roll(atom_vals, -1, axis=0)], axis=1)
        tails, heads, backs = lax.map(make_assemble(second), (field_all, ghosts, scale_rows, projectors, entry_cells, entry_slots, beside_all, potentials, base_all))
        heads = heads + jnp.roll(backs, 1, axis=0)
        head_out = finish(heads, field_all[:, :, :FACEP], potentials[:, None, :FACEP], base_all[:, :, :FACEP], second)
        return jnp.concatenate([head_out, tails], axis=2)

    first_step = apply_filter(fields, fields, False)
    filtered = apply_filter(first_step, fields, True)

    def accumulate(running, block):
        return running + jnp.dot(block, block.T, preferred_element_type=jnp.float32), None

    correlation, unused = lax.scan(accumulate, jnp.zeros((states, states), jnp.float32), filtered)
    correlation = correlation / NODES_ALL
    filtered_out = filtered.transpose(1, 0, 2).reshape(states, partitions * NODES)
    return filtered_out, correlation
```

```python
import functools

import jax
import jax.numpy as jnp
from jax import lax
from jax.experimental import pallas as pl
from jax.experimental.pallas import tpu as pltpu
from jax.sharding import PartitionSpec as P

FACEP = 1792
CENTER = 0.5
HALFWIDTH = 2.5
HIGH = lax.Precision.HIGHEST
WIDE = 256
GROUP = 12
F32 = jnp.float32
BF16 = jnp.bfloat16


def from_behind(value, axis, steps):
    count = lax.axis_size(axis)
    pairs = [(source, (source + steps) % count) for source in range(count)]
    return lax.ppermute(value, axis, pairs)


def fill_onehot(cn_ref, group, oh_ref):
    rows = cn_ref[group]
    hi = jnp.bitwise_and(rows, WIDE - 1)
    lanes = rows.shape[1]
    iota = lax.broadcasted_iota(jnp.int32, (WIDE, lanes), 0)
    for jj in range(GROUP):
        oh_ref[:, jj * lanes:(jj + 1) * lanes] = jnp.where(
            iota == hi[jj:jj + 1, :], 1.0, 0.0
        ).astype(BF16)
    return lax.shift_right_logical(rows, 8)


def gather_kernel(flags_ref, cn_ref, ext_ref, kmat_ref, scale_ref, proj_ref, ecell_ref,
                  eatom_ref, ct_ref, grouped_ref, lhs_ref, oh_ref, xs_ref, es_ref):
    states = ext_ref.shape[0]
    chunks, rows_in_chunk, _ = lhs_ref.shape
    layers = rows_in_chunk // states
    groups = cn_ref.shape[0]
    cells = cn_ref.shape[2]
    width = groups * GROUP
    for c in range(chunks):
        base = c * layers * WIDE
        parts = [
            ext_ref[:, base + l * WIDE:base + (l + 1) * WIDE].astype(F32) for l in range(layers)
        ]
        lhs_ref[c] = jnp.concatenate(parts, axis=0).astype(BF16)

    def group_body(g, carry):
        lo = fill_onehot(cn_ref, g, oh_ref)

        def chunk_body(c, inner):
            @pl.when(flags_ref[g * chunks + c] > 0)
            def _():
                out = jnp.dot(lhs_ref[c], oh_ref[...], preferred_element_type=F32)
                for jj in range(GROUP):
                    where = pl.ds(pl.multiple_of((g * GROUP + jj) * states, states), states)
                    value = xs_ref[where, :]
                    row = lo[jj:jj + 1, :] - c * layers
                    for l in range(layers):
                        value = jnp.where(
                            row == l,
                            out[l * states:(l + 1) * states, jj * cells:(jj + 1) * cells],
                            value,
                        )
                    xs_ref[where, :] = value
            return inner

        return lax.fori_loop(0, chunks, chunk_body, carry)

    xs_ref[...] = jnp.zeros_like(xs_ref)
    lax.fori_loop(0, groups, group_body, 0)

    cell_ids = lax.broadcasted_iota(jnp.int32, (cells, ecell_ref.shape[1]), 0)
    spread = jnp.where(cell_ids == ecell_ref[...], 1.0, 0.0).astype(BF16)
    es_ref[...] = jnp.dot(xs_ref[...].astype(BF16), spread, preferred_element_type=F32)

    kmat = kmat_ref[...]
    scale = scale_ref[...]
    for s in range(0, states, 2):
        pair = jnp.concatenate(
            [xs_ref[pl.ds(s, width, stride=states), :], xs_ref[pl.ds(s + 1, width, stride=states), :]],
            axis=1,
        ).astype(BF16)
        out = jnp.dot(kmat, pair, preferred_element_type=F32)
        ct_ref[pl.ds(s, width, stride=states), :] = out[:, :cells] * scale
        ct_ref[pl.ds(s + 1, width, stride=states), :] = out[:, cells:] * scale

    nproj = proj_ref.shape[1]
    entries = ecell_ref.shape[1]

    def partial_body(j, accs):
        values = es_ref[pl.ds(pl.multiple_of(j * states, states), states), :]
        proj = proj_ref[j].astype(F32)
        return tuple(acc + proj[k:k + 1, :] * values for k, acc in enumerate(accs))

    zero = jnp.zeros((states, entries), F32)
    accs = lax.fori_loop(0, width, partial_body, (zero,) * nproj, unroll=4)
    partial_sum = jnp.concatenate(accs, axis=0)
    atoms = grouped_ref.shape[2]
    slot_ids = lax.broadcasted_iota(jnp.int32, (atoms, entries), 0)
    for g in range(3):
        chosen = jnp.where(eatom_ref[...] == slot_ids + g * atoms, 1.0, 0.0)
        grouped_ref[g] = lax.dot_general(
            partial_sum, chosen, (((1,), (1,)), ((), ())), precision=HIGH,
            preferred_element_type=F32,
        )


def scatter_kernel(flags_ref, cn_ref, ct_ref, coef_ref, coup_ref, proj_ref, ecell_ref,
                   eatom_ref, y_ref, oh_ref, ns_ref, v_ref, lhs_ref, acc_ref):
    chunks, rows_in_chunk, _ = acc_ref.shape
    groups = cn_ref.shape[0]
    cells = cn_ref.shape[2]
    width = groups * GROUP
    states = ct_ref.shape[0] // width
    layers = rows_in_chunk // (2 * states)
    nproj = proj_ref.shape[1]
    entries = ecell_ref.shape[1]
    atoms = coef_ref.shape[2]
    slot_ids = lax.broadcasted_iota(jnp.int32, (atoms, entries), 0)
    entry_terms = jnp.zeros((nproj * states, entries), F32)
    for g in range(3):
        rows = []
        for k in range(nproj):
            acc = jnp.zeros((states, atoms), F32)
            for l in range(nproj):
                acc = acc + (
                    coup_ref[g, k * nproj + l:k * nproj + l + 1, :]
                    * coef_ref[g, l * states:(l + 1) * states, :]
                )
            rows.append(acc)
        chosen = jnp.where(eatom_ref[...] == slot_ids + g * atoms, 1.0, 0.0)
        entry_terms = entry_terms + jnp.dot(
            jnp.concatenate(rows, axis=0), chosen, precision=HIGH, preferred_element_type=F32
        )
    terms = [entry_terms[k * states:(k + 1) * states, :] for k in range(nproj)]

    def node_body(j, carry):
        proj = proj_ref[j].astype(F32)
        total = proj[0:1, :] * terms[0]
        for k in range(1, nproj):
            total = total + proj[k:k + 1, :] * terms[k]
        ns_ref[pl.ds(pl.multiple_of(j * states, states), states), :] = total
        return carry

    lax.fori_loop(0, width, node_body, 0, unroll=4)
    cell_ids = lax.broadcasted_iota(jnp.int32, (cells, entries), 0)
    spread = jnp.where(cell_ids == ecell_ref[...], 1.0, 0.0).astype(BF16)
    back = (((1,), (1,)), ((), ()))
    node_vals = ns_ref[...]
    node_top = node_vals.astype(BF16)
    node_rest = (node_vals - node_top.astype(F32)).astype(BF16)
    v_ref[...] = (
        ct_ref[...]
        + lax.dot_general(node_top, spread, back, preferred_element_type=F32)
        + lax.dot_general(node_rest, spread, back, preferred_element_type=F32)
    )
    acc_ref[...] = jnp.zeros_like(acc_ref)

    def group_body(g, carry):
        lo = fill_onehot(cn_ref, g, oh_ref)

        def chunk_body(c, inner):
            @pl.when(flags_ref[g * chunks + c] > 0)
            def _():
                for jj in range(GROUP):
                    start = pl.multiple_of((g * GROUP + jj) * states, states)
                    value = v_ref[pl.ds(start, states), :]
                    top = value.astype(BF16).astype(F32)
                    both = jnp.concatenate([top, value - top], axis=0)
                    row = lo[jj:jj + 1, :] - c * layers
                    for l in range(layers):
                        lhs_ref[l * 2 * states:(l + 1) * 2 * states, jj * cells:(jj + 1) * cells] = (
                            jnp.where(row == l, both, 0.0).astype(BF16)
                        )
                acc_ref[c] += lax.dot_general(
                    lhs_ref[...], oh_ref[...], back, preferred_element_type=F32
                )
            return inner

        return lax.fori_loop(0, chunks, chunk_body, carry)

    lax.fori_loop(0, groups, group_body, 0)
    for c in range(chunks):
        for l in range(layers):
            base = (c * layers + l) * WIDE
            at = l * 2 * states
            y_ref[:, base:base + WIDE] = (
                acc_ref[c, at:at + states, :] + acc_ref[c, at + states:at + 2 * states, :]
            )


def local(
    psi,
    cell_nodes,
    cell_scale,
    cell_matrix,
    node_potential,
    proj_values,
    entry_cell,
    entry_atom,
    coupling,
):
    states, node_count = psi.shape
    width, cells = cell_nodes.shape
    atoms, nproj, _ = coupling.shape
    entries = entry_atom.shape[0]
    full = node_count + FACEP
    chunks = full // FACEP
    layers = FACEP // WIDE
    groups = width // GROUP
    span = GROUP * cells

    table = cell_nodes.reshape(groups, GROUP, cells)
    owner = table // FACEP
    flags = jnp.stack(
        [jnp.any(owner == c, axis=(1, 2)) for c in range(chunks)], axis=1
    ).astype(jnp.int32).reshape(groups * chunks)
    scale_row = cell_scale.reshape(1, cells)
    ecell = entry_cell.reshape(1, entries)
    eatom = entry_atom.reshape(1, entries)
    coup = coupling.transpose(1, 2, 0).reshape(nproj * nproj, atoms)
    coup_all = jnp.stack([from_behind(coup, "mesh", 1), coup, from_behind(coup, "mesh", -1)])
    pot_ghost = from_behind(node_potential[:FACEP], "mesh", -1)
    potential = jnp.concatenate([node_potential, pot_ghost]).astype(F32) - CENTER

    vmem = pl.BlockSpec(memory_space=pltpu.VMEM)
    smem = pl.BlockSpec(memory_space=pltpu.SMEM)

    gather = pl.pallas_call(
        gather_kernel,
        out_shape=(
            jax.ShapeDtypeStruct((width * states, cells), F32),
            jax.ShapeDtypeStruct((3, nproj * states, atoms), F32),
        ),
        in_specs=[smem] + [vmem] * 7,
        out_specs=(vmem, vmem),
        scratch_shapes=[
            pltpu.VMEM((chunks, layers * states, WIDE), BF16),
            pltpu.VMEM((WIDE, span), BF16),
            pltpu.VMEM((width * states, cells), F32),
            pltpu.VMEM((width * states, entries), F32),
        ],
        name="gather_cells",
    )
    scatter = pl.pallas_call(
        scatter_kernel,
        out_shape=jax.ShapeDtypeStruct((states, full), F32),
        in_specs=[smem] + [vmem] * 7,
        out_specs=vmem,
        scratch_shapes=[
            pltpu.VMEM((WIDE, span), BF16),
            pltpu.VMEM((width * states, entries), F32),
            pltpu.VMEM((width * states, cells), F32),
            pltpu.VMEM((layers * 2 * states, span), BF16),
            pltpu.VMEM((chunks, layers * 2 * states, WIDE), F32),
        ],
        name="scatter_nodes",
    )

    def assemble(extended):
        cell_terms, grouped = gather(
            flags, table, extended, cell_matrix, scale_row, proj_values, ecell, eatom
        )
        ahead1 = from_behind(grouped[1:], "mesh", 1)
        back1 = from_behind(grouped[:2], "mesh", -1)
        ahead2 = from_behind(grouped[2], "mesh", 2)
        back2 = from_behind(grouped[0], "mesh", -2)
        coef = jnp.stack([
            ahead1[0] + ahead2 + grouped[0],
            grouped[1] + ahead1[1] + back1[0],
            back1[1] + grouped[2] + back2,
        ])
        return scatter(flags, table, cell_terms, coef, coup_all, proj_values, ecell, eatom)

    psi_ext = jnp.concatenate([psi, from_behind(psi[:, :FACEP], "mesh", -1)], axis=1)
    summed = assemble(psi_ext)
    head = summed[:, :FACEP] + from_behind(summed[:, node_count:], "mesh", 1)
    tail = summed[:, node_count:] + from_behind(summed[:, :FACEP], "mesh", -1)
    summed = jnp.concatenate([head, summed[:, FACEP:node_count], tail], axis=1)
    first = ((summed + potential * psi_ext.astype(F32)) / HALFWIDTH).astype(BF16)
    summed = assemble(first)
    head = summed[:, :FACEP] + from_behind(summed[:, node_count:], "mesh", 1)
    summed = jnp.concatenate([head, summed[:, FACEP:node_count]], axis=1)
    scaled = (summed + potential[:node_count] * first[:, :node_count].astype(F32)) / HALFWIDTH
    filtered = (2.0 * scaled - psi.astype(F32)).astype(BF16)

    scale_all = 1.0 / (lax.axis_size("mesh") * node_count)
    all_states = lax.all_gather(filtered, "band", axis=0, tiled=True)
    local_sum = lax.dot_general(
        all_states, all_states, (((1,), (1,)), ((), ())), preferred_element_type=F32
    )
    correlation = lax.psum(local_sum, "mesh") * scale_all
    return (filtered, correlation)


def solution(mesh):
    return jax.shard_map(
        local,
        mesh=mesh,
        in_specs=(
            P("band", "mesh"),
            P(),
            P("mesh"),
            P(),
            P("mesh"),
            P(None, None, "mesh"),
            P("mesh"),
            P("mesh"),
            P("mesh", None, None),
        ),
        out_specs=(P("band", "mesh"), P()),
        check_vma=False,
    )
```

```python
import jax
import jax.numpy as jnp
from jax import lax
from jax.experimental import pallas as pl
from jax.experimental.pallas import tpu as pltpu
from jax.sharding import PartitionSpec as P

FACEP = 1792
CENTER = 0.5
HALFWIDTH = 2.5
HIGH = lax.Precision.HIGHEST
WIDE = 256
GROUP = 12
F32 = jnp.float32
BF16 = jnp.bfloat16


def fill_onehot(cn_ref, group, oh_ref):
    rows = cn_ref[group]
    hi = jnp.bitwise_and(rows, WIDE - 1)
    lanes = rows.shape[1]
    iota = lax.broadcasted_iota(jnp.int32, (WIDE, lanes), 0)
    for jj in range(GROUP):
        oh_ref[:, jj * lanes:(jj + 1) * lanes] = jnp.where(
            iota == hi[jj:jj + 1, :], 1.0, 0.0
        ).astype(BF16)
    return lax.shift_right_logical(rows, 8)


def gather_kernel(flags_ref, cn_ref, ext_ref, kmat_ref, scale_ref, proj_ref, ecell_ref,
                  eatom_ref, ct_ref, grouped_ref, lhs_ref, oh_ref, xs_ref, es_ref):
    states = ext_ref.shape[0]
    chunks, rows_in_chunk, _ = lhs_ref.shape
    layers = rows_in_chunk // states
    groups = cn_ref.shape[0]
    cells = cn_ref.shape[2]
    width = groups * GROUP
    for c in range(chunks):
        base = c * layers * WIDE
        parts = [
            ext_ref[:, base + l * WIDE:base + (l + 1) * WIDE].astype(F32) for l in range(layers)
        ]
        lhs_ref[c] = jnp.concatenate(parts, axis=0).astype(BF16)

    def group_body(g, carry):
        lo = fill_onehot(cn_ref, g, oh_ref)

        def chunk_body(c, inner):
            @pl.when(flags_ref[g * chunks + c] > 0)
            def _():
                out = jnp.dot(lhs_ref[c], oh_ref[...], preferred_element_type=F32)
                for jj in range(GROUP):
                    where = pl.ds(pl.multiple_of((g * GROUP + jj) * states, states), states)
                    value = xs_ref[where, :]
                    row = lo[jj:jj + 1, :] - c * layers
                    for l in range(layers):
                        value = jnp.where(
                            row == l,
                            out[l * states:(l + 1) * states, jj * cells:(jj + 1) * cells],
                            value,
                        )
                    xs_ref[where, :] = value
            return inner

        return lax.fori_loop(0, chunks, chunk_body, carry)

    xs_ref[...] = jnp.zeros_like(xs_ref)
    lax.fori_loop(0, groups, group_body, 0)

    cell_ids = lax.broadcasted_iota(jnp.int32, (cells, ecell_ref.shape[1]), 0)
    spread = jnp.where(cell_ids == ecell_ref[...], 1.0, 0.0).astype(BF16)
    es_ref[...] = jnp.dot(xs_ref[...].astype(BF16), spread, preferred_element_type=F32)

    kmat = kmat_ref[...]
    scale = scale_ref[...]
    for s in range(0, states, 2):
        pair = jnp.concatenate(
            [xs_ref[pl.ds(s, width, stride=states), :], xs_ref[pl.ds(s + 1, width, stride=states), :]],
            axis=1,
        ).astype(BF16)
        out = jnp.dot(kmat, pair, preferred_element_type=F32)
        ct_ref[pl.ds(s, width, stride=states), :] = out[:, :cells] * scale
        ct_ref[pl.ds(s + 1, width, stride=states), :] = out[:, cells:] * scale

    nproj = proj_ref.shape[1]
    entries = ecell_ref.shape[1]

    def partial_body(j, accs):
        values = es_ref[pl.ds(pl.multiple_of(j * states, states), states), :]
        proj = proj_ref[j].astype(F32)
        return tuple(acc + proj[k:k + 1, :] * values for k, acc in enumerate(accs))

    zero = jnp.zeros((states, entries), F32)
    accs = lax.fori_loop(0, width, partial_body, (zero,) * nproj, unroll=4)
    partial_sum = jnp.concatenate(accs, axis=0)
    atoms = grouped_ref.shape[2]
    slot_ids = lax.broadcasted_iota(jnp.int32, (atoms, entries), 0)
    for g in range(3):
        chosen = jnp.where(eatom_ref[...] == slot_ids + g * atoms, 1.0, 0.0)
        grouped_ref[g] = lax.dot_general(
            partial_sum, chosen, (((1,), (1,)), ((), ())), precision=HIGH,
            preferred_element_type=F32,
        )


def scatter_kernel(flags_ref, cn_ref, ct_ref, coef_ref, coup_ref, proj_ref, ecell_ref,
                   eatom_ref, y_ref, oh_ref, ns_ref, v_ref, lhs_ref, acc_ref):
    chunks, rows_in_chunk, _ = acc_ref.shape
    groups = cn_ref.shape[0]
    cells = cn_ref.shape[2]
    width = groups * GROUP
    states = ct_ref.shape[0] // width
    layers = rows_in_chunk // (2 * states)
    nproj = proj_ref.shape[1]
    entries = ecell_ref.shape[1]
    atoms = coef_ref.shape[2]
    slot_ids = lax.broadcasted_iota(jnp.int32, (atoms, entries), 0)
    entry_terms = jnp.zeros((nproj * states, entries), F32)
    for g in range(3):
        rows = []
        for k in range(nproj):
            acc = jnp.zeros((states, atoms), F32)
            for l in range(nproj):
                acc = acc + (
                    coup_ref[g, k * nproj + l:k * nproj + l + 1, :]
                    * coef_ref[g, l * states:(l + 1) * states, :]
                )
            rows.append(acc)
        chosen = jnp.where(eatom_ref[...] == slot_ids + g * atoms, 1.0, 0.0)
        entry_terms = entry_terms + jnp.dot(
            jnp.concatenate(rows, axis=0), chosen, precision=HIGH, preferred_element_type=F32
        )
    terms = [entry_terms[k * states:(k + 1) * states, :] for k in range(nproj)]

    def node_body(j, carry):
        proj = proj_ref[j].astype(F32)
        total = proj[0:1, :] * terms[0]
        for k in range(1, nproj):
            total = total + proj[k:k + 1, :] * terms[k]
        ns_ref[pl.ds(pl.multiple_of(j * states, states), states), :] = total
        return carry

    lax.fori_loop(0, width, node_body, 0, unroll=4)
    cell_ids = lax.broadcasted_iota(jnp.int32, (cells, entries), 0)
    spread = jnp.where(cell_ids == ecell_ref[...], 1.0, 0.0).astype(BF16)
    back = (((1,), (1,)), ((), ()))
    node_vals = ns_ref[...]
    node_top = node_vals.astype(BF16)
    node_rest = (node_vals - node_top.astype(F32)).astype(BF16)
    v_ref[...] = (
        ct_ref[...]
        + lax.dot_general(node_top, spread, back, preferred_element_type=F32)
        + lax.dot_general(node_rest, spread, back, preferred_element_type=F32)
    )
    acc_ref[...] = jnp.zeros_like(acc_ref)

    def group_body(g, carry):
        lo = fill_onehot(cn_ref, g, oh_ref)

        def chunk_body(c, inner):
            @pl.when(flags_ref[g * chunks + c] > 0)
            def _():
                for jj in range(GROUP):
                    start = pl.multiple_of((g * GROUP + jj) * states, states)
                    value = v_ref[pl.ds(start, states), :]
                    top = value.astype(BF16).astype(F32)
                    both = jnp.concatenate([top, value - top], axis=0)
                    row = lo[jj:jj + 1, :] - c * layers
                    for l in range(layers):
                        lhs_ref[l * 2 * states:(l + 1) * 2 * states, jj * cells:(jj + 1) * cells] = (
                            jnp.where(row == l, both, 0.0).astype(BF16)
                        )
                acc_ref[c] += lax.dot_general(
                    lhs_ref[...], oh_ref[...], back, preferred_element_type=F32
                )
            return inner

        return lax.fori_loop(0, chunks, chunk_body, carry)

    lax.fori_loop(0, groups, group_body, 0)
    for c in range(chunks):
        for l in range(layers):
            base = (c * layers + l) * WIDE
            at = l * 2 * states
            y_ref[:, base:base + WIDE] = (
                acc_ref[c, at:at + states, :] + acc_ref[c, at + states:at + 2 * states, :]
            )


MESH_ID = pl.DeviceIdType.MESH


def ring_peer(steps):
    count = lax.axis_size("mesh")
    return lax.rem(lax.axis_index("mesh") + steps + count, count)


def send(src, dst, sems, at, peer):
    copy = pltpu.make_async_remote_copy(
        src_ref=src, dst_ref=dst, send_sem=sems.at[0, at], recv_sem=sems.at[1, at],
        device_id=peer, device_id_type=MESH_ID,
    )
    copy.start()
    return copy


def greet(peers):
    barrier = pltpu.get_barrier_semaphore()
    for peer in peers:
        pl.semaphore_signal(barrier, inc=1, device_id=peer, device_id_type=MESH_ID)
    return barrier


def start_kernel(psi_ref, pot_ref, coup_ref, ext_ref, potx_ref, coups_ref, sems):
    count = psi_ref.shape[1]
    face = ext_ref.shape[1] - count
    ahead, behind = {"mesh": ring_peer(1)}, {"mesh": ring_peer(-1)}
    pl.semaphore_wait(greet((ahead, behind)), 2)
    copies = [
        send(psi_ref.at[:, :face], ext_ref.at[:, count:], sems, 0, behind),
        send(coup_ref, coups_ref.at[0], sems, 1, ahead),
        send(coup_ref, coups_ref.at[2], sems, 2, behind),
        send(pot_ref.at[:, :face], potx_ref.at[:, count:], sems, 3, behind),
    ]
    ext_ref[:, :count] = psi_ref[...]
    potx_ref[:, :count] = pot_ref[...]
    coups_ref[1] = coup_ref[...]
    for copy in copies:
        copy.wait()


def atoms_kernel(grouped_ref, coef_ref, left_ref, right_ref, far_ref, sems):
    peers = [{"mesh": ring_peer(steps)} for steps in (1, -1, 2, -2)]
    pl.semaphore_wait(greet(peers), 4)
    copies = [
        send(grouped_ref.at[1:3], left_ref, sems, 0, peers[0]),
        send(grouped_ref.at[0:2], right_ref, sems, 1, peers[1]),
        send(grouped_ref.at[2], far_ref.at[0], sems, 2, peers[2]),
        send(grouped_ref.at[0], far_ref.at[1], sems, 3, peers[3]),
    ]
    for copy in copies:
        copy.wait()
    coef_ref[0] = left_ref[0] + far_ref[0] + grouped_ref[0]
    coef_ref[1] = grouped_ref[1] + left_ref[1] + right_ref[0]
    coef_ref[2] = right_ref[1] + grouped_ref[2] + far_ref[1]


def first_kernel(y_ref, ext_ref, pot_ref, first_ref, low_ref, high_ref, sems):
    full = y_ref.shape[1]
    face = low_ref.shape[1]
    count = full - face
    ahead, behind = {"mesh": ring_peer(1)}, {"mesh": ring_peer(-1)}
    barrier = greet((ahead, behind))

    def finish(total, at):
        scaled = (total + pot_ref[:, at] * ext_ref[:, at].astype(F32)) / HALFWIDTH
        first_ref[:, at] = scaled.astype(BF16)

    pl.semaphore_wait(barrier, 2)
    copies = [
        send(y_ref.at[:, count:], low_ref, sems, 0, ahead),
        send(y_ref.at[:, :face], high_ref, sems, 1, behind),
    ]
    for base in range(face, count, face):
        at = slice(base, base + face)
        finish(y_ref[:, at], at)
    for copy in copies:
        copy.wait()
    finish(y_ref[:, :face] + low_ref[...], slice(0, face))
    finish(y_ref[:, count:] + high_ref[...], slice(count, full))


def last_kernel(y_ref, first_ref, psi_ref, pot_ref, out_ref, corr_ref, low_ref, other_ref,
                slots_ref, sems):
    count = psi_ref.shape[1]
    face = low_ref.shape[1]
    devices = lax.axis_size("mesh")
    bands = lax.axis_size("band")
    me = lax.axis_index("mesh")
    band = lax.axis_index("band")
    partner = {"band": lax.rem(band + 1, bands)}
    barrier = greet((partner,))

    def greet_body(steps, carry):
        pl.semaphore_signal(
            barrier, inc=1, device_id={"mesh": lax.rem(me + steps, devices)}, device_id_type=MESH_ID
        )
        return carry

    lax.fori_loop(1, devices, greet_body, 0)

    def finish(total, at):
        scaled = (total + pot_ref[:, at] * first_ref[:, at].astype(F32)) / HALFWIDTH
        out_ref[:, at] = (2.0 * scaled - psi_ref[:, at].astype(F32)).astype(BF16)

    pl.semaphore_wait(barrier, devices)
    tail = send(y_ref.at[:, count:count + face], low_ref, sems, 0, {"mesh": ring_peer(1)})
    for base in range(face, count, face):
        at = slice(base, base + face)
        finish(y_ref[:, at], at)
    tail.wait()
    finish(y_ref[:, :face] + low_ref[...], slice(0, face))
    swap = send(out_ref, other_ref, sems, 1, partner)
    swap.wait()
    states = out_ref.shape[0]
    total = jnp.zeros((bands * states, bands * states), F32)
    for base in range(0, count, face):
        at = slice(base, base + face)
        own, other = out_ref[:, at].astype(F32), other_ref[:, at].astype(F32)
        block = jnp.concatenate(
            [jnp.where(band == 0, own, other), jnp.where(band == 0, other, own)], axis=0
        ).astype(BF16)
        total = total + lax.dot_general(
            block, block, (((1,), (1,)), ((), ())), preferred_element_type=F32
        )
    slots_ref[me] = total

    def push(steps, carry):
        send(slots_ref.at[me], slots_ref.at[me], sems, 2, {"mesh": lax.rem(me + steps, devices)})
        return carry

    lax.fori_loop(1, devices, push, 0)
    pltpu.make_async_remote_copy(
        src_ref=slots_ref.at[pl.ds(0, devices - 1)], dst_ref=slots_ref.at[pl.ds(0, devices - 1)],
        send_sem=sems.at[0, 2], recv_sem=sems.at[1, 2], device_id=partner, device_id_type=MESH_ID,
    ).wait()
    corr_ref[...] = jnp.sum(slots_ref[...], axis=0) * (1.0 / (devices * count))


def local(
    psi,
    cell_nodes,
    cell_scale,
    cell_matrix,
    node_potential,
    proj_values,
    entry_cell,
    entry_atom,
    coupling,
):
    states, node_count = psi.shape
    width, cells = cell_nodes.shape
    atoms, nproj, _ = coupling.shape
    entries = entry_atom.shape[0]
    full = node_count + FACEP
    chunks = full // FACEP
    layers = FACEP // WIDE
    groups = width // GROUP
    span = GROUP * cells

    table = cell_nodes.reshape(groups, GROUP, cells)
    owner = table // FACEP
    flags = jnp.stack(
        [jnp.any(owner == c, axis=(1, 2)) for c in range(chunks)], axis=1
    ).astype(jnp.int32).reshape(groups * chunks)
    scale_row = cell_scale.reshape(1, cells)
    ecell = entry_cell.reshape(1, entries)
    eatom = entry_atom.reshape(1, entries)
    coup = coupling.transpose(1, 2, 0).reshape(nproj * nproj, atoms)
    potential = node_potential.astype(F32).reshape(1, node_count) - CENTER

    vmem = pl.BlockSpec(memory_space=pltpu.VMEM)
    smem = pl.BlockSpec(memory_space=pltpu.SMEM)

    gather = pl.pallas_call(
        gather_kernel,
        out_shape=(
            jax.ShapeDtypeStruct((width * states, cells), F32),
            jax.ShapeDtypeStruct((3, nproj * states, atoms), F32),
        ),
        in_specs=[smem] + [vmem] * 7,
        out_specs=(vmem, vmem),
        scratch_shapes=[
            pltpu.VMEM((chunks, layers * states, WIDE), BF16),
            pltpu.VMEM((WIDE, span), BF16),
            pltpu.VMEM((width * states, cells), F32),
            pltpu.VMEM((width * states, entries), F32),
        ],
        name="gather_cells",
    )
    scatter = pl.pallas_call(
        scatter_kernel,
        out_shape=jax.ShapeDtypeStruct((states, full), F32),
        in_specs=[smem] + [vmem] * 7,
        out_specs=vmem,
        scratch_shapes=[
            pltpu.VMEM((WIDE, span), BF16),
            pltpu.VMEM((width * states, entries), F32),
            pltpu.VMEM((width * states, cells), F32),
            pltpu.VMEM((layers * 2 * states, span), BF16),
            pltpu.VMEM((chunks, layers * 2 * states, WIDE), F32),
        ],
        name="scatter_nodes",
    )

    def remote(kernel, outs, n_in, scratch, copies, ident):
        return pl.pallas_call(
            kernel,
            out_shape=tuple(jax.ShapeDtypeStruct(*out) for out in outs),
            in_specs=[vmem] * n_in,
            out_specs=(vmem,) * len(outs),
            scratch_shapes=[pltpu.VMEM(*one) for one in scratch]
            + [pltpu.SemaphoreType.DMA((2, copies))],
            compiler_params=pltpu.CompilerParams(collective_id=ident, has_side_effects=True),
            name=kernel.__name__,
        )

    pair = (nproj * states, atoms)

    def assemble(extended, ident):
        cell_terms, grouped = gather(
            flags, table, extended, cell_matrix, scale_row, proj_values, ecell, eatom
        )
        (coef,) = remote(
            atoms_kernel, [((3,) + pair, F32)], 1,
            [((2,) + pair, F32), ((2,) + pair, F32), ((2,) + pair, F32)], 4, ident,
        )(grouped)
        return scatter(flags, table, cell_terms, coef, coup_all, proj_values, ecell, eatom)

    psi_ext, pot_ext, coup_all = remote(
        start_kernel,
        [((states, full), BF16), ((1, full), F32), ((3, nproj * nproj, atoms), F32)],
        3, [], 4, 0,
    )(psi, potential, coup)
    face = (states, FACEP)
    (first,) = remote(first_kernel, [((states, full), BF16)], 3, [(face, F32), (face, F32)], 2, 2)(
        assemble(psi_ext, 1), psi_ext, pot_ext
    )
    bands, devices = lax.axis_size("band"), lax.axis_size("mesh")
    square = (bands * states, bands * states)
    filtered, correlation = remote(
        last_kernel,
        [((states, node_count), BF16), (square, F32)],
        4,
        [(face, F32), ((states, node_count), BF16), ((devices,) + square, F32)],
        3, 4,
    )(assemble(first, 3), first, psi, potential)
    return (filtered, correlation)


def solution(mesh):
    return jax.shard_map(
        local,
        mesh=mesh,
        in_specs=(
            P("band", "mesh"),
            P(),
            P("mesh"),
            P(),
            P("mesh"),
            P(None, None, "mesh"),
            P("mesh"),
            P("mesh"),
            P("mesh", None, None),
        ),
        out_specs=(P("band", "mesh"), P()),
        check_vma=False,
    )
```

```python
import jax
import jax.numpy as jnp
from jax import lax
from jax.experimental import pallas as pl
from jax.experimental.pallas import tpu as pltpu
from jax.sharding import PartitionSpec as P

FACEP = 1792
CENTER = 0.5
HALFWIDTH = 2.5
HIGH = lax.Precision.HIGHEST
WIDE = 256
GROUP = 12
F32 = jnp.float32
BF16 = jnp.bfloat16


def fill_onehot(cn_ref, group, oh_ref):
    rows = cn_ref[group]
    hi = jnp.bitwise_and(rows, WIDE - 1)
    lanes = rows.shape[1]
    iota = lax.broadcasted_iota(jnp.int32, (WIDE, lanes), 0)
    for jj in range(GROUP):
        oh_ref[:, jj * lanes:(jj + 1) * lanes] = jnp.where(
            iota == hi[jj:jj + 1, :], 1.0, 0.0
        ).astype(BF16)
    return lax.shift_right_logical(rows, 8)


def gather_kernel(sched_ref, cn_ref, ext_ref, xs_ref, lhs_ref, oh_ref):
    states = ext_ref.shape[0]
    chunks = lhs_ref.shape[0] - 1
    layers = ext_ref.shape[1] // (chunks * WIDE)
    groups = cn_ref.shape[0]
    cells = cn_ref.shape[2]
    padded = lhs_ref.shape[1]
    slots = sched_ref.shape[0] // groups
    lhs_ref[...] = jnp.zeros_like(lhs_ref)
    for c in range(chunks):
        base = c * layers * WIDE
        parts = [
            ext_ref[:, base + l * WIDE:base + (l + 1) * WIDE].astype(F32) for l in range(layers)
        ]
        parts.append(jnp.zeros((padded - layers * states, WIDE), F32))
        lhs_ref[c] = jnp.concatenate(parts, axis=0).astype(BF16)
    xs_ref[...] = jnp.zeros_like(xs_ref)

    def group_body(g, carry):
        lo = fill_onehot(cn_ref, g, oh_ref)

        def pair_body(r, inner):
            first = sched_ref[g * slots + 2 * r]
            second = sched_ref[g * slots + 2 * r + 1]
            lhs = jnp.concatenate([lhs_ref[first], lhs_ref[second]], axis=0)
            out = jnp.dot(lhs, oh_ref[...], preferred_element_type=F32)
            for jj in range(GROUP):
                where = pl.ds(pl.multiple_of((g * GROUP + jj) * states, states), states)
                value = xs_ref[where, :]
                lanes = slice(jj * cells, (jj + 1) * cells)
                for half, chunk in enumerate((first, second)):
                    row = lo[jj:jj + 1, :] - chunk * layers
                    for l in range(layers):
                        at = half * padded + l * states
                        value = jnp.where(row == l, out[at:at + states, lanes], value)
                xs_ref[where, :] = value
            return inner

        pairs = lax.shift_right_logical(sched_ref[g * slots + slots - 1] + 1, 1)
        return lax.fori_loop(0, pairs, pair_body, carry)

    lax.fori_loop(0, groups, group_body, 0)


def scatter_kernel(sched_ref, cn_ref, ct_ref, coef_ref, coup_ref, proj_ref, ecell_ref,
                   eatom_ref, y_ref, oh_ref, ns_ref, v_ref, lhs_ref, acc_ref):
    chunks, rows_in_chunk, _ = acc_ref.shape
    chunks = chunks - 1
    groups = cn_ref.shape[0]
    cells = cn_ref.shape[2]
    width = groups * GROUP
    states = ct_ref.shape[0] // width
    layers = rows_in_chunk // (2 * states)
    nproj = proj_ref.shape[1]
    entries = ecell_ref.shape[1]
    atoms = coef_ref.shape[2]
    slot_ids = lax.broadcasted_iota(jnp.int32, (atoms, entries), 0)
    entry_terms = jnp.zeros((nproj * states, entries), F32)
    for g in range(3):
        rows = []
        for k in range(nproj):
            acc = jnp.zeros((states, atoms), F32)
            for l in range(nproj):
                acc = acc + (
                    coup_ref[g, k * nproj + l:k * nproj + l + 1, :]
                    * coef_ref[g, l * states:(l + 1) * states, :]
                )
            rows.append(acc)
        chosen = jnp.where(eatom_ref[...] == slot_ids + g * atoms, 1.0, 0.0)
        entry_terms = entry_terms + jnp.dot(
            jnp.concatenate(rows, axis=0), chosen, precision=HIGH, preferred_element_type=F32
        )
    terms = [entry_terms[k * states:(k + 1) * states, :] for k in range(nproj)]

    def node_body(j, carry):
        proj = proj_ref[j].astype(F32)
        total = proj[0:1, :] * terms[0]
        for k in range(1, nproj):
            total = total + proj[k:k + 1, :] * terms[k]
        ns_ref[pl.ds(pl.multiple_of(j * states, states), states), :] = total
        return carry

    lax.fori_loop(0, width, node_body, 0, unroll=4)
    cell_ids = lax.broadcasted_iota(jnp.int32, (cells, entries), 0)
    spread = jnp.where(cell_ids == ecell_ref[...], 1.0, 0.0).astype(BF16)
    back = (((1,), (1,)), ((), ()))
    node_vals = ns_ref[...]
    node_top = node_vals.astype(BF16)
    node_rest = (node_vals - node_top.astype(F32)).astype(BF16)
    v_ref[...] = (
        ct_ref[...]
        + lax.dot_general(node_top, spread, back, preferred_element_type=F32)
        + lax.dot_general(node_rest, spread, back, preferred_element_type=F32)
    )
    acc_ref[...] = jnp.zeros_like(acc_ref)
    slots = sched_ref.shape[0] // groups

    def group_body(g, carry):
        lo = fill_onehot(cn_ref, g, oh_ref)

        def pair_body(r, inner):
            first = sched_ref[g * slots + 2 * r]
            second = sched_ref[g * slots + 2 * r + 1]
            for jj in range(GROUP):
                start = pl.multiple_of((g * GROUP + jj) * states, states)
                value = v_ref[pl.ds(start, states), :]
                top = value.astype(BF16).astype(F32)
                both = jnp.concatenate([top, value - top], axis=0)
                lanes = slice(jj * cells, (jj + 1) * cells)
                for half, chunk in enumerate((first, second)):
                    row = lo[jj:jj + 1, :] - chunk * layers
                    for l in range(layers):
                        at = half * rows_in_chunk + l * 2 * states
                        lhs_ref[at:at + 2 * states, lanes] = (
                            jnp.where(row == l, both, 0.0).astype(BF16)
                        )
            out = lax.dot_general(lhs_ref[...], oh_ref[...], back, preferred_element_type=F32)
            acc_ref[first] += out[:rows_in_chunk]
            acc_ref[second] += out[rows_in_chunk:]
            return inner

        pairs = lax.shift_right_logical(sched_ref[g * slots + slots - 1] + 1, 1)
        return lax.fori_loop(0, pairs, pair_body, carry)

    lax.fori_loop(0, groups, group_body, 0)
    for c in range(chunks):
        for l in range(layers):
            base = (c * layers + l) * WIDE
            at = l * 2 * states
            y_ref[:, base:base + WIDE] = (
                acc_ref[c, at:at + states, :] + acc_ref[c, at + states:at + 2 * states, :]
            )


MESH_ID = pl.DeviceIdType.MESH


def ring_peer(steps):
    count = lax.axis_size("mesh")
    return lax.rem(lax.axis_index("mesh") + steps + count, count)


def send(src, dst, sems, at, peer):
    copy = pltpu.make_async_remote_copy(
        src_ref=src, dst_ref=dst, send_sem=sems.at[0, at], recv_sem=sems.at[1, at],
        device_id=peer, device_id_type=MESH_ID,
    )
    copy.start()
    return copy


def greet(peers):
    barrier = pltpu.get_barrier_semaphore()
    for peer in peers:
        pl.semaphore_signal(barrier, inc=1, device_id=peer, device_id_type=MESH_ID)
    return barrier


def start_kernel(psi_ref, pot_ref, coup_ref, ext_ref, potx_ref, coups_ref, sems):
    count = psi_ref.shape[1]
    face = ext_ref.shape[1] - count
    ahead, behind = {"mesh": ring_peer(1)}, {"mesh": ring_peer(-1)}
    pl.semaphore_wait(greet((ahead, behind)), 2)
    copies = [
        send(psi_ref.at[:, :face], ext_ref.at[:, count:], sems, 0, behind),
        send(coup_ref, coups_ref.at[0], sems, 1, ahead),
        send(coup_ref, coups_ref.at[2], sems, 2, behind),
        send(pot_ref.at[:, :face], potx_ref.at[:, count:], sems, 3, behind),
    ]
    ext_ref[:, :count] = psi_ref[...]
    potx_ref[:, :count] = pot_ref[...]
    coups_ref[1] = coup_ref[...]
    for copy in copies:
        copy.wait()


def atoms_kernel(xs_ref, kmat_ref, scale_ref, proj_ref, ecell_ref, eatom_ref, ct_ref, coef_ref,
                 es_ref, grouped_ref, left_ref, right_ref, far_ref, sems):
    peers = [{"mesh": ring_peer(steps)} for steps in (1, -1, 2, -2)]
    barrier = greet(peers)
    width, nproj, entries = proj_ref.shape
    cells = xs_ref.shape[1]
    states = xs_ref.shape[0] // width
    cell_ids = lax.broadcasted_iota(jnp.int32, (cells, entries), 0)
    spread = jnp.where(cell_ids == ecell_ref[...], 1.0, 0.0).astype(BF16)
    es_ref[...] = jnp.dot(xs_ref[...].astype(BF16), spread, preferred_element_type=F32)

    def partial_body(j, accs):
        values = es_ref[pl.ds(pl.multiple_of(j * states, states), states), :]
        proj = proj_ref[j].astype(F32)
        return tuple(acc + proj[k:k + 1, :] * values for k, acc in enumerate(accs))

    zero = jnp.zeros((states, entries), F32)
    accs = lax.fori_loop(0, width, partial_body, (zero,) * nproj, unroll=4)
    partial_sum = jnp.concatenate(accs, axis=0)
    atoms = grouped_ref.shape[2]
    slot_ids = lax.broadcasted_iota(jnp.int32, (atoms, entries), 0)
    for g in range(3):
        chosen = jnp.where(eatom_ref[...] == slot_ids + g * atoms, 1.0, 0.0)
        grouped_ref[g] = lax.dot_general(
            partial_sum, chosen, (((1,), (1,)), ((), ())), precision=HIGH,
            preferred_element_type=F32,
        )
    pl.semaphore_wait(barrier, 4)
    copies = [
        send(grouped_ref.at[1:3], left_ref, sems, 0, peers[0]),
        send(grouped_ref.at[0:2], right_ref, sems, 1, peers[1]),
        send(grouped_ref.at[2], far_ref.at[0], sems, 2, peers[2]),
        send(grouped_ref.at[0], far_ref.at[1], sems, 3, peers[3]),
    ]
    kmat = kmat_ref[...]
    scale = scale_ref[...]
    for s in range(0, states, 2):
        pair = jnp.concatenate(
            [xs_ref[pl.ds(s, width, stride=states), :], xs_ref[pl.ds(s + 1, width, stride=states), :]],
            axis=1,
        ).astype(BF16)
        out = jnp.dot(kmat, pair, preferred_element_type=F32)
        ct_ref[pl.ds(s, width, stride=states), :] = out[:, :cells] * scale
        ct_ref[pl.ds(s + 1, width, stride=states), :] = out[:, cells:] * scale
    for copy in copies:
        copy.wait()
    coef_ref[0] = left_ref[0] + far_ref[0] + grouped_ref[0]
    coef_ref[1] = grouped_ref[1] + left_ref[1] + right_ref[0]
    coef_ref[2] = right_ref[1] + grouped_ref[2] + far_ref[1]


def first_kernel(y_ref, ext_ref, pot_ref, first_ref, low_ref, high_ref, sems):
    full = y_ref.shape[1]
    face = low_ref.shape[1]
    count = full - face
    ahead, behind = {"mesh": ring_peer(1)}, {"mesh": ring_peer(-1)}
    barrier = greet((ahead, behind))

    def finish(total, at):
        scaled = (total + pot_ref[:, at] * ext_ref[:, at].astype(F32)) / HALFWIDTH
        first_ref[:, at] = scaled.astype(BF16)

    middle = face * (1 + (count // face - 1) // 2)
    for base in range(face, middle, face):
        at = slice(base, base + face)
        finish(y_ref[:, at], at)
    pl.semaphore_wait(barrier, 2)
    copies = [
        send(y_ref.at[:, count:], low_ref, sems, 0, ahead),
        send(y_ref.at[:, :face], high_ref, sems, 1, behind),
    ]
    for base in range(middle, count, face):
        at = slice(base, base + face)
        finish(y_ref[:, at], at)
    for copy in copies:
        copy.wait()
    finish(y_ref[:, :face] + low_ref[...], slice(0, face))
    finish(y_ref[:, count:] + high_ref[...], slice(count, full))


def last_kernel(y_ref, first_ref, psi_ref, pot_ref, out_ref, corr_ref, low_ref, other_ref,
                slots_ref, sems):
    count = psi_ref.shape[1]
    face = low_ref.shape[1]
    devices = lax.axis_size("mesh")
    bands = lax.axis_size("band")
    me = lax.axis_index("mesh")
    band = lax.axis_index("band")
    partner = {"band": lax.rem(band + 1, bands)}
    barrier = greet((partner,))

    def greet_body(steps, carry):
        pl.semaphore_signal(
            barrier, inc=1, device_id={"mesh": lax.rem(me + steps, devices)}, device_id_type=MESH_ID
        )
        return carry

    lax.fori_loop(1, devices, greet_body, 0)

    def finish(total, at):
        scaled = (total + pot_ref[:, at] * first_ref[:, at].astype(F32)) / HALFWIDTH
        out_ref[:, at] = (2.0 * scaled - psi_ref[:, at].astype(F32)).astype(BF16)

    for base in range(face, count, face):
        at = slice(base, base + face)
        finish(y_ref[:, at], at)
    pl.semaphore_wait(barrier, devices)
    tail = send(y_ref.at[:, count:count + face], low_ref, sems, 0, {"mesh": ring_peer(1)})
    swap = send(out_ref.at[:, face:], other_ref.at[:, face:], sems, 1, partner)
    states = out_ref.shape[0]

    def gram(base):
        at = slice(base, base + face)
        own, other = out_ref[:, at].astype(F32), other_ref[:, at].astype(F32)
        block = jnp.concatenate(
            [jnp.where(band == 0, own, other), jnp.where(band == 0, other, own)], axis=0
        ).astype(BF16)
        return lax.dot_general(
            block, block, (((1,), (1,)), ((), ())), preferred_element_type=F32
        )

    tail.wait()
    finish(y_ref[:, :face] + low_ref[...], slice(0, face))
    edge = send(out_ref.at[:, :face], other_ref.at[:, :face], sems, 3, partner)
    swap.wait()
    total = gram(face)
    for base in range(2 * face, count, face):
        total = total + gram(base)
    edge.wait()
    total = total + gram(0)
    slots_ref[me] = total

    def push(steps, carry):
        send(slots_ref.at[me], slots_ref.at[me], sems, 2, {"mesh": lax.rem(me + steps, devices)})
        return carry

    lax.fori_loop(1, devices, push, 0)
    pltpu.make_async_remote_copy(
        src_ref=slots_ref.at[pl.ds(0, devices - 1)], dst_ref=slots_ref.at[pl.ds(0, devices - 1)],
        send_sem=sems.at[0, 2], recv_sem=sems.at[1, 2], device_id=partner, device_id_type=MESH_ID,
    ).wait()
    corr_ref[...] = jnp.sum(slots_ref[...], axis=0) * (1.0 / (devices * count))


def local(
    psi,
    cell_nodes,
    cell_scale,
    cell_matrix,
    node_potential,
    proj_values,
    entry_cell,
    entry_atom,
    coupling,
):
    states, node_count = psi.shape
    width, cells = cell_nodes.shape
    atoms, nproj, _ = coupling.shape
    entries = entry_atom.shape[0]
    full = node_count + FACEP
    chunks = full // FACEP
    layers = FACEP // WIDE
    groups = width // GROUP
    span = GROUP * cells

    table = cell_nodes.reshape(groups, GROUP, cells)
    owner = table // FACEP
    flags = jnp.stack(
        [jnp.any(owner == c, axis=(1, 2)) for c in range(chunks)], axis=1
    ).astype(jnp.int32)
    ids = jnp.arange(chunks, dtype=jnp.int32)
    rank = jnp.sum(flags[:, None, :] * (ids[None, :] < ids[:, None]), axis=2)
    places = jnp.arange(chunks + 1, dtype=jnp.int32)
    used = flags[:, :, None] * (rank[:, :, None] == places)
    listed = chunks + jnp.sum(used * (ids[None, :, None] - chunks), axis=1)
    listed = jnp.concatenate(
        [listed, jnp.full((groups, 1), chunks, jnp.int32), jnp.sum(flags, axis=1, keepdims=True)],
        axis=1,
    )
    sched = listed.astype(jnp.int32).reshape(groups * (chunks + 3))
    scale_row = cell_scale.reshape(1, cells)
    ecell = entry_cell.reshape(1, entries)
    eatom = entry_atom.reshape(1, entries)
    coup = coupling.transpose(1, 2, 0).reshape(nproj * nproj, atoms)
    potential = node_potential.astype(F32).reshape(1, node_count) - CENTER

    vmem = pl.BlockSpec(memory_space=pltpu.VMEM)
    smem = pl.BlockSpec(memory_space=pltpu.SMEM)

    padded = (layers * states + 15) // 16 * 16
    gather = pl.pallas_call(
        gather_kernel,
        out_shape=jax.ShapeDtypeStruct((width * states, cells), F32),
        in_specs=[smem] + [vmem] * 2,
        out_specs=vmem,
        scratch_shapes=[
            pltpu.VMEM((chunks + 1, padded, WIDE), BF16),
            pltpu.VMEM((WIDE, span), BF16),
        ],
        name="gather_cells",
    )
    scatter = pl.pallas_call(
        scatter_kernel,
        out_shape=jax.ShapeDtypeStruct((states, full), F32),
        in_specs=[smem] + [vmem] * 7,
        out_specs=vmem,
        scratch_shapes=[
            pltpu.VMEM((WIDE, span), BF16),
            pltpu.VMEM((width * states, entries), F32),
            pltpu.VMEM((width * states, cells), F32),
            pltpu.VMEM((2 * layers * 2 * states, span), BF16),
            pltpu.VMEM((chunks + 1, layers * 2 * states, WIDE), F32),
        ],
        name="scatter_nodes",
    )

    def remote(kernel, outs, n_in, scratch, copies, ident):
        return pl.pallas_call(
            kernel,
            out_shape=tuple(jax.ShapeDtypeStruct(*out) for out in outs),
            in_specs=[vmem] * n_in,
            out_specs=(vmem,) * len(outs),
            scratch_shapes=[pltpu.VMEM(*one) for one in scratch]
            + [pltpu.SemaphoreType.DMA((2, copies))],
            compiler_params=pltpu.CompilerParams(collective_id=ident, has_side_effects=True),
            name=kernel.__name__,
        )

    pair = (nproj * states, atoms)

    def assemble(extended, ident):
        values = gather(sched, table, extended)
        cell_terms, coef = remote(
            atoms_kernel, [((width * states, cells), F32), ((3,) + pair, F32)], 6,
            [((width * states, entries), F32), ((3,) + pair, F32)] + [((2,) + pair, F32)] * 3,
            4, ident,
        )(values, cell_matrix, scale_row, proj_values, ecell, eatom)
        return scatter(sched, table, cell_terms, coef, coup_all, proj_values, ecell, eatom)

    psi_ext, pot_ext, coup_all = remote(
        start_kernel,
        [((states, full), BF16), ((1, full), F32), ((3, nproj * nproj, atoms), F32)],
        3, [], 4, 0,
    )(psi, potential, coup)
    face = (states, FACEP)
    (first,) = remote(first_kernel, [((states, full), BF16)], 3, [(face, F32), (face, F32)], 2, 2)(
        assemble(psi_ext, 1), psi_ext, pot_ext
    )
    bands, devices = lax.axis_size("band"), lax.axis_size("mesh")
    square = (bands * states, bands * states)
    filtered, correlation = remote(
        last_kernel,
        [((states, node_count), BF16), (square, F32)],
        4,
        [(face, F32), ((states, node_count), BF16), ((devices,) + square, F32)],
        4, 4,
    )(assemble(first, 3), first, psi, potential)
    return (filtered, correlation)


def solution(mesh):
    return jax.shard_map(
        local,
        mesh=mesh,
        in_specs=(
            P("band", "mesh"),
            P(),
            P("mesh"),
            P(),
            P("mesh"),
            P(None, None, "mesh"),
            P("mesh"),
            P("mesh"),
            P("mesh", None, None),
        ),
        out_specs=(P("band", "mesh"), P()),
        check_vma=False,
    )
```

```python
import jax
import jax.numpy as jnp
from jax import lax
from jax.experimental import pallas as pl
from jax.experimental.pallas import tpu as pltpu
from jax.sharding import PartitionSpec as P

FACEP = 1792
CENTER = 0.5
HALFWIDTH = 2.5
HIGH = lax.Precision.HIGHEST
WIDE = 256
GROUP = 36
F32 = jnp.float32
BF16 = jnp.bfloat16


def fill_onehot(cn_ref, group, oh_ref):
    rows = cn_ref[group]
    hi = jnp.bitwise_and(rows, WIDE - 1)
    lanes = rows.shape[1]
    iota = lax.broadcasted_iota(jnp.int32, (WIDE, lanes), 0)
    for jj in range(GROUP):
        oh_ref[:, jj * lanes:(jj + 1) * lanes] = jnp.where(
            iota == hi[jj:jj + 1, :], 1.0, 0.0
        ).astype(BF16)
    return lax.shift_right_logical(rows, 8)


def gather_kernel(sched_ref, cn_ref, ext_ref, xs_ref, lhs_ref, oh_ref):
    states = ext_ref.shape[0]
    chunks = lhs_ref.shape[0] - 1
    layers = ext_ref.shape[1] // (chunks * WIDE)
    groups = cn_ref.shape[0]
    cells = cn_ref.shape[2]
    padded = lhs_ref.shape[1]
    slots = sched_ref.shape[0] // groups
    lhs_ref[...] = jnp.zeros_like(lhs_ref)
    for c in range(chunks):
        base = c * layers * WIDE
        parts = [
            ext_ref[:, base + l * WIDE:base + (l + 1) * WIDE].astype(F32) for l in range(layers)
        ]
        parts.append(jnp.zeros((padded - layers * states, WIDE), F32))
        lhs_ref[c] = jnp.concatenate(parts, axis=0).astype(BF16)
    xs_ref[...] = jnp.zeros_like(xs_ref)

    def group_body(g, carry):
        lo = fill_onehot(cn_ref, g, oh_ref)

        def pair_body(r, inner):
            first = sched_ref[g * slots + 2 * r]
            second = sched_ref[g * slots + 2 * r + 1]
            lhs = jnp.concatenate([lhs_ref[first], lhs_ref[second]], axis=0)
            out = jnp.dot(lhs, oh_ref[...], preferred_element_type=F32)
            for jj in range(GROUP):
                where = pl.ds(pl.multiple_of((g * GROUP + jj) * states, states), states)
                value = xs_ref[where, :]
                lanes = slice(jj * cells, (jj + 1) * cells)
                for half, chunk in enumerate((first, second)):
                    row = lo[jj:jj + 1, :] - chunk * layers
                    for l in range(layers):
                        at = half * padded + l * states
                        value = jnp.where(row == l, out[at:at + states, lanes], value)
                xs_ref[where, :] = value
            return inner

        pairs = lax.shift_right_logical(sched_ref[g * slots + slots - 1] + 1, 1)
        return lax.fori_loop(0, pairs, pair_body, carry)

    lax.fori_loop(0, groups, group_body, 0)


def scatter_kernel(sched_ref, cn_ref, ct_ref, coef_ref, coup_ref, proj_ref, ecell_ref,
                   eatom_ref, y_ref, oh_ref, ns_ref, v_ref, lhs_ref, acc_ref):
    chunks, rows_in_chunk, _ = acc_ref.shape
    chunks = chunks - 1
    groups = cn_ref.shape[0]
    cells = cn_ref.shape[2]
    width = groups * GROUP
    states = ct_ref.shape[0] // width
    layers = rows_in_chunk // (2 * states)
    nproj = proj_ref.shape[1]
    entries = ecell_ref.shape[1]
    atoms = coef_ref.shape[2]
    slot_ids = lax.broadcasted_iota(jnp.int32, (atoms, entries), 0)
    entry_terms = jnp.zeros((nproj * states, entries), F32)
    for g in range(3):
        rows = []
        for k in range(nproj):
            acc = jnp.zeros((states, atoms), F32)
            for l in range(nproj):
                acc = acc + (
                    coup_ref[g, k * nproj + l:k * nproj + l + 1, :]
                    * coef_ref[g, l * states:(l + 1) * states, :]
                )
            rows.append(acc)
        chosen = jnp.where(eatom_ref[...] == slot_ids + g * atoms, 1.0, 0.0)
        entry_terms = entry_terms + jnp.dot(
            jnp.concatenate(rows, axis=0), chosen, precision=HIGH, preferred_element_type=F32
        )
    terms = [entry_terms[k * states:(k + 1) * states, :] for k in range(nproj)]

    def node_body(j, carry):
        proj = proj_ref[j].astype(F32)
        total = proj[0:1, :] * terms[0]
        for k in range(1, nproj):
            total = total + proj[k:k + 1, :] * terms[k]
        ns_ref[pl.ds(pl.multiple_of(j * states, states), states), :] = total
        return carry

    lax.fori_loop(0, width, node_body, 0, unroll=8)
    cell_ids = lax.broadcasted_iota(jnp.int32, (cells, entries), 0)
    spread = jnp.where(cell_ids == ecell_ref[...], 1.0, 0.0).astype(BF16)
    back = (((1,), (1,)), ((), ()))
    node_vals = ns_ref[...]
    node_top = node_vals.astype(BF16)
    node_rest = (node_vals - node_top.astype(F32)).astype(BF16)
    v_ref[...] = (
        ct_ref[...]
        + lax.dot_general(node_top, spread, back, preferred_element_type=F32)
        + lax.dot_general(node_rest, spread, back, preferred_element_type=F32)
    )
    acc_ref[...] = jnp.zeros_like(acc_ref)
    slots = sched_ref.shape[0] // groups

    def group_body(g, carry):
        lo = fill_onehot(cn_ref, g, oh_ref)

        def pair_body(r, inner):
            first = sched_ref[g * slots + 2 * r]
            second = sched_ref[g * slots + 2 * r + 1]
            for jj in range(GROUP):
                start = pl.multiple_of((g * GROUP + jj) * states, states)
                value = v_ref[pl.ds(start, states), :]
                top = value.astype(BF16).astype(F32)
                both = jnp.concatenate([top, value - top], axis=0)
                lanes = slice(jj * cells, (jj + 1) * cells)
                for half, chunk in enumerate((first, second)):
                    row = lo[jj:jj + 1, :] - chunk * layers
                    for l in range(layers):
                        at = half * rows_in_chunk + l * 2 * states
                        lhs_ref[at:at + 2 * states, lanes] = (
                            jnp.where(row == l, both, 0.0).astype(BF16)
                        )
            out = lax.dot_general(lhs_ref[...], oh_ref[...], back, preferred_element_type=F32)
            acc_ref[first] += out[:rows_in_chunk]
            acc_ref[second] += out[rows_in_chunk:]
            return inner

        pairs = lax.shift_right_logical(sched_ref[g * slots + slots - 1] + 1, 1)
        return lax.fori_loop(0, pairs, pair_body, carry)

    lax.fori_loop(0, groups, group_body, 0)
    for c in range(chunks):
        for l in range(layers):
            base = (c * layers + l) * WIDE
            at = l * 2 * states
            y_ref[:, base:base + WIDE] = (
                acc_ref[c, at:at + states, :] + acc_ref[c, at + states:at + 2 * states, :]
            )


MESH_ID = pl.DeviceIdType.MESH


def ring_peer(steps):
    count = lax.axis_size("mesh")
    return lax.rem(lax.axis_index("mesh") + steps + count, count)


def send(src, dst, sems, at, peer):
    copy = pltpu.make_async_remote_copy(
        src_ref=src, dst_ref=dst, send_sem=sems.at[0, at], recv_sem=sems.at[1, at],
        device_id=peer, device_id_type=MESH_ID,
    )
    copy.start()
    return copy


def greet(peers):
    barrier = pltpu.get_barrier_semaphore()
    for peer in peers:
        pl.semaphore_signal(barrier, inc=1, device_id=peer, device_id_type=MESH_ID)
    return barrier


def start_kernel(psi_ref, pot_ref, coup_ref, ext_ref, potx_ref, coups_ref, sems):
    count = psi_ref.shape[1]
    face = ext_ref.shape[1] - count
    ahead, behind = {"mesh": ring_peer(1)}, {"mesh": ring_peer(-1)}
    pl.semaphore_wait(greet((ahead, behind)), 2)
    copies = [
        send(psi_ref.at[:, :face], ext_ref.at[:, count:], sems, 0, behind),
        send(coup_ref, coups_ref.at[0], sems, 1, ahead),
        send(coup_ref, coups_ref.at[2], sems, 2, behind),
        send(pot_ref.at[:, :face], potx_ref.at[:, count:], sems, 3, behind),
    ]
    ext_ref[:, :count] = psi_ref[...]
    potx_ref[:, :count] = pot_ref[...]
    coups_ref[1] = coup_ref[...]
    for copy in copies:
        copy.wait()


def atoms_kernel(xs_ref, kmat_ref, scale_ref, proj_ref, ecell_ref, eatom_ref, ct_ref, coef_ref,
                 es_ref, grouped_ref, left_ref, right_ref, far_ref, sems):
    peers = [{"mesh": ring_peer(steps)} for steps in (1, -1, 2, -2)]
    barrier = greet(peers)
    width, nproj, entries = proj_ref.shape
    cells = xs_ref.shape[1]
    states = xs_ref.shape[0] // width
    cell_ids = lax.broadcasted_iota(jnp.int32, (cells, entries), 0)
    spread = jnp.where(cell_ids == ecell_ref[...], 1.0, 0.0).astype(BF16)
    es_ref[...] = jnp.dot(xs_ref[...].astype(BF16), spread, preferred_element_type=F32)

    def partial_body(j, accs):
        values = es_ref[pl.ds(pl.multiple_of(j * states, states), states), :]
        proj = proj_ref[j].astype(F32)
        return tuple(acc + proj[k:k + 1, :] * values for k, acc in enumerate(accs))

    zero = jnp.zeros((states, entries), F32)
    accs = lax.fori_loop(0, width, partial_body, (zero,) * nproj, unroll=8)
    partial_sum = jnp.concatenate(accs, axis=0)
    atoms = grouped_ref.shape[2]
    slot_ids = lax.broadcasted_iota(jnp.int32, (atoms, entries), 0)
    for g in range(3):
        chosen = jnp.where(eatom_ref[...] == slot_ids + g * atoms, 1.0, 0.0)
        grouped_ref[g] = lax.dot_general(
            partial_sum, chosen, (((1,), (1,)), ((), ())), precision=HIGH,
            preferred_element_type=F32,
        )
    pl.semaphore_wait(barrier, 4)
    copies = [
        send(grouped_ref.at[1:3], left_ref, sems, 0, peers[0]),
        send(grouped_ref.at[0:2], right_ref, sems, 1, peers[1]),
        send(grouped_ref.at[2], far_ref.at[0], sems, 2, peers[2]),
        send(grouped_ref.at[0], far_ref.at[1], sems, 3, peers[3]),
    ]
    kmat = kmat_ref[...]
    scale = scale_ref[...]
    for s in range(0, states, 2):
        pair = jnp.concatenate(
            [xs_ref[pl.ds(s, width, stride=states), :], xs_ref[pl.ds(s + 1, width, stride=states), :]],
            axis=1,
        ).astype(BF16)
        out = jnp.dot(kmat, pair, preferred_element_type=F32)
        ct_ref[pl.ds(s, width, stride=states), :] = out[:, :cells] * scale
        ct_ref[pl.ds(s + 1, width, stride=states), :] = out[:, cells:] * scale
    for copy in copies:
        copy.wait()
    coef_ref[0] = left_ref[0] + far_ref[0] + grouped_ref[0]
    coef_ref[1] = grouped_ref[1] + left_ref[1] + right_ref[0]
    coef_ref[2] = right_ref[1] + grouped_ref[2] + far_ref[1]


def first_kernel(y_ref, ext_ref, pot_ref, first_ref, low_ref, high_ref, sems):
    full = y_ref.shape[1]
    face = low_ref.shape[1]
    count = full - face
    ahead, behind = {"mesh": ring_peer(1)}, {"mesh": ring_peer(-1)}
    barrier = greet((ahead, behind))

    def finish(total, at):
        scaled = (total + pot_ref[:, at] * ext_ref[:, at].astype(F32)) / HALFWIDTH
        first_ref[:, at] = scaled.astype(BF16)

    middle = face * (1 + (count // face - 1) // 2)
    for base in range(face, middle, face):
        at = slice(base, base + face)
        finish(y_ref[:, at], at)
    pl.semaphore_wait(barrier, 2)
    copies = [
        send(y_ref.at[:, count:], low_ref, sems, 0, ahead),
        send(y_ref.at[:, :face], high_ref, sems, 1, behind),
    ]
    for base in range(middle, count, face):
        at = slice(base, base + face)
        finish(y_ref[:, at], at)
    for copy in copies:
        copy.wait()
    finish(y_ref[:, :face] + low_ref[...], slice(0, face))
    finish(y_ref[:, count:] + high_ref[...], slice(count, full))


def last_kernel(y_ref, first_ref, psi_ref, pot_ref, out_ref, corr_ref, low_ref, other_ref,
                slots_ref, sems):
    count = psi_ref.shape[1]
    face = low_ref.shape[1]
    devices = lax.axis_size("mesh")
    bands = lax.axis_size("band")
    me = lax.axis_index("mesh")
    band = lax.axis_index("band")
    partner = {"band": lax.rem(band + 1, bands)}
    barrier = greet((partner,))

    def greet_body(steps, carry):
        pl.semaphore_signal(
            barrier, inc=1, device_id={"mesh": lax.rem(me + steps, devices)}, device_id_type=MESH_ID
        )
        return carry

    lax.fori_loop(1, devices, greet_body, 0)

    def finish(total, at):
        scaled = (total + pot_ref[:, at] * first_ref[:, at].astype(F32)) / HALFWIDTH
        out_ref[:, at] = (2.0 * scaled - psi_ref[:, at].astype(F32)).astype(BF16)

    for base in range(face, count, face):
        at = slice(base, base + face)
        finish(y_ref[:, at], at)
    pl.semaphore_wait(barrier, devices)
    tail = send(y_ref.at[:, count:count + face], low_ref, sems, 0, {"mesh": ring_peer(1)})
    swap = send(out_ref.at[:, face:], other_ref.at[:, face:], sems, 1, partner)
    states = out_ref.shape[0]

    def gram(base):
        at = slice(base, base + face)
        own, other = out_ref[:, at].astype(F32), other_ref[:, at].astype(F32)
        block = jnp.concatenate(
            [jnp.where(band == 0, own, other), jnp.where(band == 0, other, own)], axis=0
        ).astype(BF16)
        return lax.dot_general(
            block, block, (((1,), (1,)), ((), ())), preferred_element_type=F32
        )

    swap.wait()
    total = gram(face)
    for base in range(2 * face, count, face):
        total = total + gram(base)
    tail.wait()
    finish(y_ref[:, :face] + low_ref[...], slice(0, face))
    edge = send(out_ref.at[:, :face], other_ref.at[:, :face], sems, 3, partner)
    edge.wait()
    total = total + gram(0)
    slots_ref[me] = total

    def push(steps, carry):
        send(slots_ref.at[me], slots_ref.at[me], sems, 2, {"mesh": lax.rem(me + steps, devices)})
        return carry

    lax.fori_loop(1, devices, push, 0)
    pltpu.make_async_remote_copy(
        src_ref=slots_ref.at[pl.ds(0, devices - 1)], dst_ref=slots_ref.at[pl.ds(0, devices - 1)],
        send_sem=sems.at[0, 2], recv_sem=sems.at[1, 2], device_id=partner, device_id_type=MESH_ID,
    ).wait()
    corr_ref[...] = jnp.sum(slots_ref[...], axis=0) * (1.0 / (devices * count))


def local(
    psi,
    cell_nodes,
    cell_scale,
    cell_matrix,
    node_potential,
    proj_values,
    entry_cell,
    entry_atom,
    coupling,
):
    states, node_count = psi.shape
    width, cells = cell_nodes.shape
    atoms, nproj, _ = coupling.shape
    entries = entry_atom.shape[0]
    full = node_count + FACEP
    chunks = full // FACEP
    layers = FACEP // WIDE
    groups = width // GROUP
    span = GROUP * cells

    table = cell_nodes.reshape(groups, GROUP, cells)
    owner = table // FACEP
    flags = jnp.stack(
        [jnp.any(owner == c, axis=(1, 2)) for c in range(chunks)], axis=1
    ).astype(jnp.int32)
    ids = jnp.arange(chunks, dtype=jnp.int32)
    rank = jnp.sum(flags[:, None, :] * (ids[None, :] < ids[:, None]), axis=2)
    places = jnp.arange(chunks + 1, dtype=jnp.int32)
    used = flags[:, :, None] * (rank[:, :, None] == places)
    listed = chunks + jnp.sum(used * (ids[None, :, None] - chunks), axis=1)
    listed = jnp.concatenate(
        [listed, jnp.full((groups, 1), chunks, jnp.int32), jnp.sum(flags, axis=1, keepdims=True)],
        axis=1,
    )
    sched = listed.astype(jnp.int32).reshape(groups * (chunks + 3))
    scale_row = cell_scale.reshape(1, cells)
    ecell = entry_cell.reshape(1, entries)
    eatom = entry_atom.reshape(1, entries)
    coup = coupling.transpose(1, 2, 0).reshape(nproj * nproj, atoms)
    potential = node_potential.astype(F32).reshape(1, node_count) - CENTER

    vmem = pl.BlockSpec(memory_space=pltpu.VMEM)
    smem = pl.BlockSpec(memory_space=pltpu.SMEM)

    padded = (layers * states + 15) // 16 * 16
    gather = pl.pallas_call(
        gather_kernel,
        out_shape=jax.ShapeDtypeStruct((width * states, cells), F32),
        in_specs=[smem] + [vmem] * 2,
        out_specs=vmem,
        scratch_shapes=[
            pltpu.VMEM((chunks + 1, padded, WIDE), BF16),
            pltpu.VMEM((WIDE, span), BF16),
        ],
        name="gather_cells",
    )
    scatter = pl.pallas_call(
        scatter_kernel,
        out_shape=jax.ShapeDtypeStruct((states, full), F32),
        in_specs=[smem] + [vmem] * 7,
        out_specs=vmem,
        scratch_shapes=[
            pltpu.VMEM((WIDE, span), BF16),
            pltpu.VMEM((width * states, entries), F32),
            pltpu.VMEM((width * states, cells), F32),
            pltpu.VMEM((2 * layers * 2 * states, span), BF16),
            pltpu.VMEM((chunks + 1, layers * 2 * states, WIDE), F32),
        ],
        name="scatter_nodes",
    )

    def remote(kernel, outs, n_in, scratch, copies, ident):
        return pl.pallas_call(
            kernel,
            out_shape=tuple(jax.ShapeDtypeStruct(*out) for out in outs),
            in_specs=[vmem] * n_in,
            out_specs=(vmem,) * len(outs),
            scratch_shapes=[pltpu.VMEM(*one) for one in scratch]
            + [pltpu.SemaphoreType.DMA((2, copies))],
            compiler_params=pltpu.CompilerParams(collective_id=ident, has_side_effects=True),
            name=kernel.__name__,
        )

    pair = (nproj * states, atoms)

    def assemble(extended, ident):
        values = gather(sched, table, extended)
        cell_terms, coef = remote(
            atoms_kernel, [((width * states, cells), F32), ((3,) + pair, F32)], 6,
            [((width * states, entries), F32), ((3,) + pair, F32)] + [((2,) + pair, F32)] * 3,
            4, ident,
        )(values, cell_matrix, scale_row, proj_values, ecell, eatom)
        return scatter(sched, table, cell_terms, coef, coup_all, proj_values, ecell, eatom)

    psi_ext, pot_ext, coup_all = remote(
        start_kernel,
        [((states, full), BF16), ((1, full), F32), ((3, nproj * nproj, atoms), F32)],
        3, [], 4, 0,
    )(psi, potential, coup)
    face = (states, FACEP)
    (first,) = remote(first_kernel, [((states, full), BF16)], 3, [(face, F32), (face, F32)], 2, 2)(
        assemble(psi_ext, 1), psi_ext, pot_ext
    )
    bands, devices = lax.axis_size("band"), lax.axis_size("mesh")
    square = (bands * states, bands * states)
    filtered, correlation = remote(
        last_kernel,
        [((states, node_count), BF16), (square, F32)],
        4,
        [(face, F32), ((states, node_count), BF16), ((devices,) + square, F32)],
        4, 4,
    )(assemble(first, 3), first, psi, potential)
    return (filtered, correlation)


def solution(mesh):
    return jax.shard_map(
        local,
        mesh=mesh,
        in_specs=(
            P("band", "mesh"),
            P(),
            P("mesh"),
            P(),
            P("mesh"),
            P(None, None, "mesh"),
            P("mesh"),
            P("mesh"),
            P("mesh", None, None),
        ),
        out_specs=(P("band", "mesh"), P()),
        check_vma=False,
    )
```
